512 devices in a mesh: gy: 64 (over z, x, core), gz: 8 (over y).
Axes of the slice: x: 4, y: 8, z: 8, core: 2. Of those that a mesh axis runs over, the one named last changes fastest.
Arguments:
- velocity: float32 [3, 1536, 4096], P(None, ('gy', 'gz')), may hold values from -6 to 6
- explicit: float32 [3, 1536, 4096], P(None, ('gy', 'gz')), may hold values from -6 to 6
- bands: float32 [2, 5, 1536], P(None, None, 'gy'), may hold values from -0.6 to 0.6
- inverse: float32 [1536, 24, 2048], P('gy', None, 'gz'), may hold values from -1.25 to 1.25
- spikes: float32 [2, 2, 1536, 2048], P(None, None, 'gy', 'gz'), may hold values from -1.4 to 1.4
Outputs:
- updated: float32 [3, 1536, 4096], P(None, 'gy', 'gz')
The draws below stay inside these ranges and needn't reach their ends.
All inputs are finite; a program needn't handle non-finite values.
Results may differ from the reference program's by a relative error of at most 0.00024.
Values sent between devices are 32-bit elements; how exact they have to be, the bound alone decides.
A program may use at most 64 MiB of HBM per device.

```python
import math
import jax
import jax.numpy as jnp
from jax import lax

NYD = 24
NY = 1536
MODES = 2048


def draw_spikes(key, part):
    base_key = jax.random.fold_in(key, 11)
    angle_key = jax.random.fold_in(key, 12)
    decay_key = jax.random.fold_in(key, 13)
    blocks = NY // NYD
    filler = jnp.clip(0.35 * jax.random.normal(base_key, (2, 2, NY, MODES), jnp.float32), -1.4, 1.4)
    low_rate = -1.0 / 10.0
    high_rate = -1.0 / 32.0
    angles = jax.random.uniform(angle_key, (2, blocks, MODES), jnp.float32, -math.pi, math.pi)
    radius = jnp.exp(jax.random.uniform(decay_key, (2, blocks, MODES), jnp.float32, low_rate, high_rate))
    cosine = jnp.repeat(radius * jnp.cos(angles), NYD, axis=1)
    sine_part = jnp.repeat(radius * jnp.sin(angles), NYD, axis=1)
    within = jnp.arange(NY) % NYD
    first_row = jnp.stack([within == NYD - 2, within == 0])
    second_row = jnp.stack([within == NYD - 1, within == 1])
    at_first = jnp.stack([cosine, -sine_part], axis=1)
    at_second = jnp.stack([sine_part, cosine], axis=1)
    result = jnp.where(first_row[:, None, :, None], at_first, filler)
    result = jnp.where(second_row[:, None, :, None], at_second, result)
    return result.astype(jnp.float32)


def shard_levels(key, extent, split, low, top_value):
    level, own = 1.0, jax.random.fold_in(key, 6)
    for position, blocks in split:
        draws = jnp.exp(jax.random.uniform(jax.random.fold_in(own, position), (blocks,), jnp.float32, low / len(split), top_value / len(split)))
        level = level * jnp.repeat(draws, extent[position] // blocks).reshape([-1 if axis == position else 1 for axis in range(len(extent))])
    return level


def scatter_about(rng, shape, width, reach, cuts=(), dtype=jnp.bfloat16):
    array = width * jax.random.normal(rng, shape, jnp.float32)
    if cuts:
        array = array * shard_levels(rng, shape, cuts, -0.22, 0.18)
    return jnp.clip(array, -reach, reach).astype(dtype)


def setup_inputs(seed: int = 0) -> dict:
    keys = jax.random.split(jax.random.key(seed), 6)
    velocity = scatter_about(keys[0], (3, NY, 2 * MODES), 1.0, 6.0, ((1, 512),), jnp.float32)
    explicit = scatter_about(keys[1], (3, NY, 2 * MODES), 1.0, 6.0, ((1, 512),), jnp.float32)
    bands = jnp.clip(jax.random.uniform(keys[2], (2, 5, NY), jnp.float32, -0.6, 0.6) * shard_levels(keys[2], (2, 5, NY), ((2, 64),), -0.4, 0.0), -0.6, 0.6)
    inverse = scatter_about(keys[3], (NY, NYD, MODES), NYD ** -0.5, 1.25, ((0, 64), (2, 8)), jnp.float32)
    spikes = draw_spikes(jax.random.fold_in(keys[5], 71), 0)
    return {"velocity": velocity, "explicit": explicit, "bands": bands, "inverse": inverse, "spikes": spikes}


def couple(spike, state):
    first = spike[..., 0, :, :][..., None, :, :, None] * state[..., :, 0, :, :][..., :, None, :, :]
    second = spike[..., 1, :, :][..., None, :, :, None] * state[..., :, 1, :, :][..., :, None, :, :]
    return first + second


def reference(velocity, explicit, bands, inverse, spikes):
    rows = velocity.shape[1]
    blocks = rows // NYD
    modes = inverse.shape[2]
    total = velocity + explicit
    pad_total = jnp.pad(total, ((0, 0), (2, 2), (0, 0)))
    pad_vel = jnp.pad(velocity, ((0, 0), (2, 2), (0, 0)))
    rhs = jnp.zeros(velocity.shape, jnp.float32)
    for offset in range(5):
        rhs = rhs + bands[0, offset][None, :, None] * pad_total[:, offset:offset + rows]
        rhs = rhs + bands[1, offset][None, :, None] * pad_vel[:, offset:offset + rows]
    rhs_blocks = rhs.reshape(3, blocks, NYD, modes, 2).transpose(1, 0, 2, 3, 4)
    inv_blocks = inverse.reshape(blocks, NYD, NYD, modes)
    lower = spikes[0].reshape(2, blocks, NYD, modes).transpose(1, 0, 2, 3)
    upper = spikes[1].reshape(2, blocks, NYD, modes).transpose(1, 0, 2, 3)

    def solve_block(pair):
        return jnp.einsum("rcm,fcmp->frmp", pair[0], pair[1], precision=lax.Precision.HIGHEST)

    local = lax.map(solve_block, (inv_blocks, rhs_blocks))

    def forward(state, pieces):
        zval = pieces[1] - couple(pieces[0], state)
        return zval[:, NYD - 2:], zval

    start = jnp.zeros((3, 2, modes, 2), jnp.float32)
    _, zvals = lax.scan(forward, start, (lower, local))

    def backward(state, pieces):
        xval = pieces[1] - couple(pieces[0], state)
        return xval[:, 0:2], xval

    _, xvals = lax.scan(backward, start, (upper, zvals), reverse=True)
    return xvals.transpose(1, 0, 2, 3, 4).reshape(3, rows, 2 * modes)
```

```python
import functools

import jax
import jax.numpy as jnp
from jax import lax
from jax.experimental import pallas as pl
from jax.experimental.pallas import tpu as pltpu
from jax.sharding import PartitionSpec as P

MESH = pl.DeviceIdType.MESH
F32 = jnp.float32


def kernel(
    vel, exp, bands, inv, spk, out,
    rv, re, hv, he, inv_h, inv_t, spk_h, spk_d, coef, vx, ex, rhs, local,
    map_s, map_r, gmap_s, gmap_r, cd_s, cd_r, gcd_s, gcd_r, ts_s, ts_r,
    base_t, base_s, base_r, zero_t, zero_s, t_in, s_in,
    ld_sem, own_sem, rv_send, rv_recv, re_send, re_recv, h_send, h_recv,
    m_send, m_recv, gm_send, gm_recv, c_send, c_recv, gc_send, gc_recv, ts_send, ts_recv,
):
    gy = lax.axis_index("gy")
    gz = lax.axis_index("gz")
    zi = gy // 8
    pi = gy % 8
    xj = pi // 2
    co = pi % 2

    def to_y(k):
        return {"gz": (gz + k) % 8}

    def to_plane(k):
        return {"gy": zi * 8 + (pi + k) % 8}

    def to_z(k):
        return {"gy": ((zi + k) % 8) * 8 + pi}

    def to_next(k):
        return {"gy": (gy + k + 64) % 64}

    def remote(src, dst, send, recv, where):
        return pltpu.make_async_remote_copy(
            src_ref=src, dst_ref=dst, send_sem=send, recv_sem=recv,
            device_id=where, device_id_type=MESH,
        )

    loads = []
    for h in range(2):
        loads.append(pltpu.make_async_copy(spk.at[:, pl.ds(h * 128, 128)], spk_h.at[h], ld_sem.at[h]))
    for h in range(2):
        loads.append(pltpu.make_async_copy(inv.at[:, pl.ds(h * 128, 128)], inv_h.at[h], ld_sem.at[2 + h]))
    for copy in loads:
        copy.start()
    mine = pl.ds(pl.multiple_of(gz * 512, 512), 512)
    own_v = pltpu.make_async_copy(vel.at[:, :, mine], rv.at[gz], rv_recv.at[0])
    own_e = pltpu.make_async_copy(exp.at[:, :, mine], re.at[gz], re_recv.at[0])
    own_v.start()
    own_e.start()

    barrier = pltpu.get_barrier_semaphore()
    for k in range(1, 8):
        for where in (to_y(k), to_z(k), to_plane(k)):
            pl.semaphore_signal(barrier, inc=1, device_id=where, device_id_type=MESH)
    for k in (-1, 1):
        pl.semaphore_signal(barrier, inc=1, device_id=to_next(k), device_id_type=MESH)
    pl.semaphore_wait(barrier, 23)

    sends = []
    for k in (4, 3, 5, 2, 6, 1, 7):
        cols = pl.ds(pl.multiple_of(((gz + k) % 8) * 512, 512), 512)
        for src, dst, send, recv in ((vel, rv, rv_send, rv_recv), (exp, re, re_send, re_recv)):
            copy = remote(src.at[:, :, cols], dst.at[gz], send.at[k], recv.at[k], to_y(k))
            copy.start()
            sends.append(copy)

    lane = lax.broadcasted_iota(jnp.int32, (24, 128), 1) // 2
    for h in range(2):
        loads[h].wait()

    def double_spikes(i, carry):
        row = pl.multiple_of(i * 24, 8)
        for h in range(2):
            part = spk_h[h, pl.ds(row, 24), :]
            for j in range(2):
                spk_d[2 * h + j, pl.ds(row, 24), :] = jnp.take_along_axis(part, lane + 64 * j, axis=1)
        return carry

    lax.fori_loop(0, 4, double_spikes, 0)
    for lt in range(4):
        for k in range(2):
            for q in range(2):
                i = 2 * k + q
                map_s[lt, i : i + 1, :] = -spk_d[lt, q * 24 + 22 + k : q * 24 + 23 + k, :]
                map_s[lt, 4 + i : 5 + i, :] = -spk_d[lt, q * 24 + k : q * 24 + k + 1, :]
                map_s[lt, 8 + i : 9 + i, :] = -spk_d[lt, 48 + q * 24 + k : 48 + q * 24 + k + 1, :]
    map_r[pi] = map_s[xj]
    for k in range(1, 8):
        copy = remote(
            map_s.at[(pi + k) % 8 // 2], map_r.at[pi], m_send.at[k], m_recv.at[k], to_plane(k)
        )
        copy.start()
        sends.append(copy)

    eye = lax.broadcasted_iota(jnp.int32, (24, 24), 0) == lax.broadcasted_iota(jnp.int32, (24, 24), 1)
    for d in range(5):
        first = bands[d : d + 1, :]
        second = bands[5 + d : 6 + d, :]
        for i, row in ((d, first + second), (5 + d, first)):
            column = jnp.sum(jnp.where(eye, row, 0.0), axis=1, keepdims=True)
            coef[i] = jnp.broadcast_to(column, (24, 128))

    for h in range(2):
        loads[2 + h].wait()

    def turn(c, carry):
        for h in range(2):
            part = inv_h[h, pl.ds(c, 24, stride=24), :]
            for j in range(2):
                inv_t[2 * h + j, c] = jnp.take_along_axis(part, lane + 64 * j, axis=1)
        return carry

    lax.fori_loop(0, 24, turn, 0)

    def apply2(maps, at, first, second):
        return (
            maps[at : at + 1, :] * first + maps[at + 1 : at + 2, :] * second,
            maps[at + 2 : at + 3, :] * first + maps[at + 3 : at + 4, :] * second,
        )

    for k in range(1, 8):
        remote(map_s.at[0], map_r.at[(pi - k + 8) % 8], m_send.at[k], m_recv.at[k], to_plane(k)).wait_recv()
    col = lax.broadcasted_iota(jnp.int32, (2, 128), 0)
    unit = (jnp.where(col == 0, 1.0, 0.0), jnp.where(col == 1, 1.0, 0.0))
    t0, t1 = unit
    for b in range(8):
        base_t[b, 0:2] = t0
        base_t[b, 2:4] = t1
        t0, t1 = apply2(map_r[b], 0, t0, t1)
    s0 = s1 = jnp.zeros((2, 128), F32)
    r0, r1 = unit
    gmap_s[0:2] = t0
    gmap_s[2:4] = t1
    for b in range(7, -1, -1):
        maps = map_r[b]
        base_s[b, 0:2] = s0
        base_s[b, 2:4] = s1
        base_r[b, 0:2] = r0
        base_r[b, 2:4] = r1
        w0, w1 = apply2(maps, 4, base_t[b, 0:2], base_t[b, 2:4])
        u0, u1 = apply2(maps, 8, s0, s1)
        s0, s1 = w0 + u0, w1 + u1
        r0, r1 = apply2(maps, 8, r0, r1)
    gmap_s[4:6] = s0
    gmap_s[6:8] = s1
    gmap_s[8:10] = r0
    gmap_s[10:12] = r1
    gmap_r[zi] = gmap_s[...]
    for k in range(1, 8):
        copy = remote(gmap_s, gmap_r.at[zi], gm_send.at[k], gm_recv.at[k], to_z(k))
        copy.start()
        sends.append(copy)

    own_v.wait()
    own_e.wait()
    for k in range(1, 8):
        slot = (gz - k + 8) % 8
        cols = pl.ds(0, 512)
        remote(vel.at[:, :, cols], rv.at[slot], rv_send.at[k], rv_recv.at[k], to_y(k)).wait_recv()
        remote(exp.at[:, :, cols], re.at[slot], re_send.at[k], re_recv.at[k], to_y(k)).wait_recv()
    halos = []
    for side, slot, step in ((0, 7, 1), (1, 0, -1)):
        for a, (src, dst) in enumerate(((rv, hv), (re, he))):
            i = 2 * side + a
            copy = remote(src.at[slot], dst.at[side], h_send.at[i], h_recv.at[i], to_next(step))
            copy.start()
            sends.append(copy)
            halos.append(copy)

    def gather_rows(lt, carry):
        cols = pl.ds(pl.multiple_of(lt * 128, 128), 128)
        for got, rows in ((rv, vx), (re, ex)):
            for g in range(8):
                for f in range(3):
                    rows[lt, f, 2 + 3 * g : 5 + 3 * g, :] = got[g, f, :, cols]
        return carry

    lax.fori_loop(0, 4, gather_rows, 0)
    for copy in halos:
        copy.wait_recv()

    def gather_edges(lt, carry):
        cols = pl.ds(pl.multiple_of(lt * 128, 128), 128)
        for got, rows in ((hv, vx), (he, ex)):
            for f in range(3):
                rows[lt, f, 0:2, :] = jnp.where(gy > 0, got[0, f, 1:3, cols], 0.0)
                rows[lt, f, 26:28, :] = jnp.where(gy < 63, got[1, f, 0:2, cols], 0.0)
        return carry

    lax.fori_loop(0, 4, gather_edges, 0)

    def solve(lt, carry):
        for f in range(3):
            total = jnp.zeros((24, 128), F32)
            for d in range(5):
                total = total + coef[d] * vx[lt, f, d : d + 24, :]
                total = total + coef[5 + d] * ex[lt, f, d : d + 24, :]
            rhs[lt, f] = total
        sums = [jnp.zeros((24, 128), F32) for _ in range(3)]
        for c in range(24):
            weight = inv_t[lt, c]
            for f in range(3):
                sums[f] = sums[f] + weight * rhs[lt, f, c : c + 1, :]
        for f in range(3):
            local[lt, f] = sums[f]
            for k in range(2):
                cd_s[lt, 3 * k + f : 3 * k + f + 1, :] = sums[f][22 + k : 23 + k, :]
                cd_s[lt, 6 + 3 * k + f : 7 + 3 * k + f, :] = sums[f][k : k + 1, :]
        return carry

    lax.fori_loop(0, 4, solve, 0)

    for k in range(1, 8):
        copy = remote(
            cd_s.at[(pi + k) % 8 // 2], cd_r.at[pi], c_send.at[k], c_recv.at[k], to_plane(k)
        )
        copy.start()
        sends.append(copy)
    cd_r[pi] = cd_s[xj]
    for k in range(1, 8):
        remote(gmap_s, gmap_r.at[(zi - k + 8) % 8], gm_send.at[k], gm_recv.at[k], to_z(k)).wait_recv()
    for k in range(1, 8):
        remote(cd_s.at[0], cd_r.at[(pi - k + 8) % 8], c_send.at[k], c_recv.at[k], to_plane(k)).wait_recv()
    t0 = t1 = jnp.zeros((3, 128), F32)
    for b in range(8):
        zero_t[b, 0:3] = t0
        zero_t[b, 3:6] = t1
        n0, n1 = apply2(map_r[b], 0, t0, t1)
        t0, t1 = n0 + cd_r[b, 0:3, :], n1 + cd_r[b, 3:6, :]
    gcd_s[0:3] = t0
    gcd_s[3:6] = t1
    s0 = s1 = jnp.zeros((3, 128), F32)
    for b in range(7, -1, -1):
        zero_s[b, 0:3] = s0
        zero_s[b, 3:6] = s1
        w0, w1 = apply2(map_r[b], 4, zero_t[b, 0:3], zero_t[b, 3:6])
        u0, u1 = apply2(map_r[b], 8, s0, s1)
        s0, s1 = u0 + (w0 + cd_r[b, 6:9, :]), u1 + (w1 + cd_r[b, 9:12, :])
    gcd_s[6:9] = s0
    gcd_s[9:12] = s1

    for k in range(1, 8):
        copy = remote(gcd_s, gcd_r.at[zi], gc_send.at[k], gc_recv.at[k], to_z(k))
        copy.start()
        sends.append(copy)
    gcd_r[zi] = gcd_s[...]
    for k in range(1, 8):
        remote(gcd_s, gcd_r.at[(zi - k + 8) % 8], gc_send.at[k], gc_recv.at[k], to_z(k)).wait_recv()
    t0 = t1 = jnp.zeros((3, 128), F32)
    for g in range(8):
        t_in[g, 0:3] = t0
        t_in[g, 3:6] = t1
        n0, n1 = apply2(gmap_r[g], 0, t0, t1)
        t0, t1 = n0 + gcd_r[g, 0:3, :], n1 + gcd_r[g, 3:6, :]
    s0 = s1 = jnp.zeros((3, 128), F32)
    for g in range(7, -1, -1):
        s_in[g, 0:3] = s0
        s_in[g, 3:6] = s1
        w0, w1 = apply2(gmap_r[g], 4, t_in[g, 0:3], t_in[g, 3:6])
        u0, u1 = apply2(gmap_r[g], 8, s0, s1)
        s0, s1 = u0 + (w0 + gcd_r[g, 6:9, :]), u1 + (w1 + gcd_r[g, 9:12, :])

    t0, t1 = t_in[zi, 0:3], t_in[zi, 3:6]
    s0, s1 = s_in[zi, 0:3], s_in[zi, 3:6]

    def mapped(base, b, first, second):
        return (
            base[b, 0:1] * first + base[b, 1:2] * second,
            base[b, 2:3] * first + base[b, 3:4] * second,
        )

    for b in range(8):
        a0, a1 = mapped(base_t, b, t0, t1)
        ts_s[b, 0:3] = zero_t[b, 0:3] + a0
        ts_s[b, 3:6] = zero_t[b, 3:6] + a1
        a0, a1 = mapped(base_s, b, t0, t1)
        b0, b1 = mapped(base_r, b, s0, s1)
        ts_s[b, 6:9] = zero_s[b, 0:3] + a0 + b0
        ts_s[b, 9:12] = zero_s[b, 3:6] + a1 + b1
    backs = []
    for k in range(1, 4):
        copy = remote(
            ts_s.at[(pi + 2 * k) % 8], ts_r.at[xj], ts_send.at[k], ts_recv.at[k], to_plane(2 * k)
        )
        copy.start()
        sends.append(copy)
    ts_r[xj] = ts_s[pi]
    for k in range(1, 4):
        remote(
            ts_s.at[0], ts_r.at[(xj - k + 4) % 4], ts_send.at[k], ts_recv.at[k], to_plane(2 * k)
        ).wait_recv()

    for lt in range(4):
        for f in range(3):
            value = local[lt, f]
            for k in range(2):
                value = value - spk_d[lt, k * 24 : k * 24 + 24, :] * ts_r[lt, 3 * k + f : 3 * k + f + 1, :]
            for k in range(2):
                value = value - spk_d[lt, 48 + k * 24 : 72 + k * 24, :] * ts_r[lt, 6 + 3 * k + f : 7 + 3 * k + f, :]
            out[f, :, lt * 128 : lt * 128 + 128] = value
    for copy in sends:
        copy.wait_send()


def per_device(velocity, explicit, bands, inverse, spikes):
    dma = pltpu.SemaphoreType.DMA
    vmem = lambda *shape: pltpu.VMEM(shape, F32)
    hbm = pl.BlockSpec(memory_space=pl.ANY)
    return pl.pallas_call(
        kernel,
        out_shape=jax.ShapeDtypeStruct((3, 24, 512), F32),
        in_specs=[hbm, hbm, pl.BlockSpec(memory_space=pltpu.VMEM), hbm, hbm],
        out_specs=pl.BlockSpec(memory_space=pltpu.VMEM),
        scratch_shapes=[
            vmem(8, 3, 3, 512), vmem(8, 3, 3, 512), vmem(2, 3, 3, 512), vmem(2, 3, 3, 512),
            vmem(2, 576, 128), vmem(4, 24, 24, 128), vmem(2, 96, 128), vmem(4, 96, 128),
            vmem(10, 24, 128), vmem(4, 3, 32, 128), vmem(4, 3, 32, 128),
            vmem(4, 3, 24, 128), vmem(4, 3, 24, 128),
            vmem(4, 12, 128), vmem(8, 12, 128), vmem(12, 128), vmem(8, 12, 128),
            vmem(4, 12, 128), vmem(8, 12, 128), vmem(12, 128), vmem(8, 12, 128),
            vmem(8, 12, 128), vmem(4, 12, 128),
            vmem(8, 4, 128), vmem(8, 4, 128), vmem(8, 4, 128),
            vmem(8, 6, 128), vmem(8, 6, 128), vmem(8, 6, 128), vmem(8, 6, 128),
            dma((4,)), dma((2,)), dma((8,)), dma((8,)), dma((8,)), dma((8,)), dma((4,)), dma((4,)),
            dma((8,)), dma((8,)), dma((8,)), dma((8,)), dma((8,)), dma((8,)), dma((8,)), dma((8,)),
            dma((4,)), dma((4,)),
        ],
        compiler_params=pltpu.CompilerParams(collective_id=0, has_side_effects=True),
    )(velocity, explicit, bands.reshape(10, 24), inverse.reshape(576, 256), spikes.reshape(96, 256))


def solution(mesh):
    placed = (
        P(None, ("gy", "gz"), None),
        P(None, ("gy", "gz"), None),
        P(None, None, "gy"),
        P("gy", None, "gz"),
        P(None, None, "gy", "gz"),
    )
    return jax.shard_map(
        per_device, mesh=mesh, in_specs=placed, out_specs=P(None, "gy", "gz"), check_vma=False
    )
```

```python
import functools

import jax
import jax.numpy as jnp
from jax import lax
from jax.experimental import pallas as pl
from jax.experimental.pallas import tpu as pltpu
from jax.sharding import PartitionSpec as P

MESH = pl.DeviceIdType.MESH
F32 = jnp.float32


def kernel(
    vel, exp, bands_in, inv, spk, out,
    bands, rv, re, hv, he, inv_h, inv_t, spk_h, spk_d, coef, vx, ex, rhs, local,
    map_s, map_r, gmap_s, gmap_r, cd_s, cd_r, gcd_s, gcd_r, ts_s, ts_r,
    base_t, base_s, base_r, zero_t, zero_s, t_in, s_in,
    ld_sem, own_sem, rv_send, rv_recv, re_send, re_recv, h_send, h_recv,
    m_send, m_recv, gm_send, gm_recv, c_send, c_recv, gc_send, gc_recv, ts_send, ts_recv,
):
    gy = lax.axis_index("gy")
    gz = lax.axis_index("gz")
    zi = gy // 8
    pi = gy % 8
    xj = pi // 2
    co = pi % 2

    def to_y(k):
        return {"gz": (gz + k) % 8}

    def to_plane(k):
        return {"gy": zi * 8 + (pi + k) % 8}

    def to_z(k):
        return {"gy": ((zi + k) % 8) * 8 + pi}

    def to_next(k):
        return {"gy": (gy + k + 64) % 64}

    def remote(src, dst, send, recv, where):
        return pltpu.make_async_remote_copy(
            src_ref=src, dst_ref=dst, send_sem=send, recv_sem=recv,
            device_id=where, device_id_type=MESH,
        )

    loads = []
    for h in range(2):
        loads.append(pltpu.make_async_copy(spk.at[:, pl.ds(h * 128, 128)], spk_h.at[h], ld_sem.at[h]))
    for h in range(2):
        loads.append(pltpu.make_async_copy(inv.at[:, pl.ds(h * 128, 128)], inv_h.at[h], ld_sem.at[2 + h]))
    loads.append(pltpu.make_async_copy(bands_in, bands, ld_sem.at[4]))
    for copy in loads:
        copy.start()
    mine = pl.ds(pl.multiple_of(gz * 512, 512), 512)
    own_v = pltpu.make_async_copy(vel.at[:, :, mine], rv.at[gz], rv_recv.at[0])
    own_e = pltpu.make_async_copy(exp.at[:, :, mine], re.at[gz], re_recv.at[0])
    own_v.start()
    own_e.start()

    barrier = pltpu.get_barrier_semaphore()
    for k in range(1, 8):
        for where in (to_y(k), to_z(k), to_plane(k)):
            pl.semaphore_signal(barrier, inc=1, device_id=where, device_id_type=MESH)
    for k in (-1, 1):
        pl.semaphore_signal(barrier, inc=1, device_id=to_next(k), device_id_type=MESH)
    pl.semaphore_wait(barrier, 23)

    sends = []
    for k in (4, 3, 5, 2, 6, 1, 7):
        cols = pl.ds(pl.multiple_of(((gz + k) % 8) * 512, 512), 512)
        for src, dst, send, recv in ((vel, rv, rv_send, rv_recv), (exp, re, re_send, re_recv)):
            copy = remote(src.at[:, :, cols], dst.at[gz], send.at[k], recv.at[k], to_y(k))
            copy.start()
            sends.append(copy)

    lane = lax.broadcasted_iota(jnp.int32, (24, 128), 1) // 2
    for h in range(2):
        loads[h].wait()

    def double_spikes(i, carry):
        row = pl.multiple_of(i * 24, 8)
        for h in range(2):
            part = spk_h[h, pl.ds(row, 24), :]
            for j in range(2):
                spk_d[2 * h + j, pl.ds(row, 24), :] = jnp.take_along_axis(part, lane + 64 * j, axis=1)
        return carry

    lax.fori_loop(0, 4, double_spikes, 0)
    for lt in range(4):
        for k in range(2):
            for q in range(2):
                i = 2 * k + q
                map_s[lt, i : i + 1, :] = -spk_d[lt, q * 24 + 22 + k : q * 24 + 23 + k, :]
                map_s[lt, 4 + i : 5 + i, :] = -spk_d[lt, q * 24 + k : q * 24 + k + 1, :]
                map_s[lt, 8 + i : 9 + i, :] = -spk_d[lt, 48 + q * 24 + k : 48 + q * 24 + k + 1, :]
    map_r[pi] = map_s[xj]
    for k in range(1, 8):
        copy = remote(
            map_s.at[(pi + k) % 8 // 2], map_r.at[pi], m_send.at[k], m_recv.at[k], to_plane(k)
        )
        copy.start()
        sends.append(copy)

    eye = lax.broadcasted_iota(jnp.int32, (24, 24), 0) == lax.broadcasted_iota(jnp.int32, (24, 24), 1)
    loads[4].wait()
    for d in range(5):
        first = bands[d, 0:1, :]
        second = bands[d, 1:2, :]
        for i, row in ((d, first + second), (5 + d, first)):
            column = jnp.sum(jnp.where(eye, row, 0.0), axis=1, keepdims=True)
            coef[i] = jnp.broadcast_to(column, (24, 128))

    def apply2(maps, at, first, second):
        return (
            maps[at : at + 1, :] * first + maps[at + 1 : at + 2, :] * second,
            maps[at + 2 : at + 3, :] * first + maps[at + 3 : at + 4, :] * second,
        )

    for k in range(1, 8):
        remote(map_s.at[0], map_r.at[(pi - k + 8) % 8], m_send.at[k], m_recv.at[k], to_plane(k)).wait_recv()
    col = lax.broadcasted_iota(jnp.int32, (2, 128), 0)
    unit = (jnp.where(col == 0, 1.0, 0.0), jnp.where(col == 1, 1.0, 0.0))
    t0, t1 = unit
    for b in range(8):
        base_t[b, 0:2] = t0
        base_t[b, 2:4] = t1
        t0, t1 = apply2(map_r[b], 0, t0, t1)
    s0 = s1 = jnp.zeros((2, 128), F32)
    r0, r1 = unit
    gmap_s[0:2] = t0
    gmap_s[2:4] = t1
    for b in range(7, -1, -1):
        maps = map_r[b]
        base_s[b, 0:2] = s0
        base_s[b, 2:4] = s1
        base_r[b, 0:2] = r0
        base_r[b, 2:4] = r1
        w0, w1 = apply2(maps, 4, base_t[b, 0:2], base_t[b, 2:4])
        u0, u1 = apply2(maps, 8, s0, s1)
        s0, s1 = w0 + u0, w1 + u1
        r0, r1 = apply2(maps, 8, r0, r1)
    gmap_s[4:6] = s0
    gmap_s[6:8] = s1
    gmap_s[8:10] = r0
    gmap_s[10:12] = r1
    gmap_r[zi] = gmap_s[...]
    for k in range(1, 8):
        copy = remote(gmap_s, gmap_r.at[zi], gm_send.at[k], gm_recv.at[k], to_z(k))
        copy.start()
        sends.append(copy)

    def wait_slot(slot):
        k = (gz - slot + 8) % 8
        pltpu.make_async_copy(rv.at[slot], rv.at[slot], rv_recv.at[k]).wait()
        pltpu.make_async_copy(re.at[slot], re.at[slot], re_recv.at[k]).wait()

    halos = []
    for side, slot, step in ((0, 7, 1), (1, 0, -1)):
        wait_slot(slot)
        for a, (src, dst) in enumerate(((rv, hv), (re, he))):
            i = 2 * side + a
            copy = remote(src.at[slot], dst.at[side], h_send.at[i], h_recv.at[i], to_next(step))
            copy.start()
            sends.append(copy)
            halos.append(copy)

    for h in range(2):
        loads[2 + h].wait()

    def turn(c, carry):
        for h in range(2):
            part = inv_h[h, pl.ds(c, 24, stride=24), :]
            for j in range(2):
                inv_t[2 * h + j, c] = jnp.take_along_axis(part, lane + 64 * j, axis=1)
        return carry

    lax.fori_loop(0, 24, turn, 0)

    def gather_rows(g):
        def body(lt, carry):
            cols = pl.ds(pl.multiple_of(lt * 128, 128), 128)
            for got, rows in ((rv, vx), (re, ex)):
                for f in range(3):
                    rows[lt, f, 2 + 3 * g : 5 + 3 * g, :] = got[g, f, :, cols]
            return carry

        lax.fori_loop(0, 4, body, 0)

    gather_rows(7)
    gather_rows(0)
    for g in (3, 4, 2, 5, 1, 6):
        wait_slot(g)
        gather_rows(g)
    for copy in halos:
        copy.wait_recv()

    def gather_edges(lt, carry):
        cols = pl.ds(pl.multiple_of(lt * 128, 128), 128)
        for got, rows in ((hv, vx), (he, ex)):
            for f in range(3):
                rows[lt, f, 0:2, :] = jnp.where(gy > 0, got[0, f, 1:3, cols], 0.0)
                rows[lt, f, 26:28, :] = jnp.where(gy < 63, got[1, f, 0:2, cols], 0.0)
        return carry

    lax.fori_loop(0, 4, gather_edges, 0)

    def solve(lt, carry):
        for f in range(3):
            total = jnp.zeros((24, 128), F32)
            for d in range(5):
                total = total + coef[d] * vx[lt, f, d : d + 24, :]
                total = total + coef[5 + d] * ex[lt, f, d : d + 24, :]
            rhs[lt, f] = total
        sums = [jnp.zeros((24, 128), F32) for _ in range(3)]
        for c in range(24):
            weight = inv_t[lt, c]
            for f in range(3):
                sums[f] = sums[f] + weight * rhs[lt, f, c : c + 1, :]
        for f in range(3):
            local[lt, f] = sums[f]
            for k in range(2):
                cd_s[lt, 3 * k + f : 3 * k + f + 1, :] = sums[f][22 + k : 23 + k, :]
                cd_s[lt, 6 + 3 * k + f : 7 + 3 * k + f, :] = sums[f][k : k + 1, :]
        return carry

    lax.fori_loop(0, 4, solve, 0)

    for k in range(1, 8):
        copy = remote(
            cd_s.at[(pi + k) % 8 // 2], cd_r.at[pi], c_send.at[k], c_recv.at[k], to_plane(k)
        )
        copy.start()
        sends.append(copy)
    cd_r[pi] = cd_s[xj]
    for k in range(1, 8):
        remote(gmap_s, gmap_r.at[(zi - k + 8) % 8], gm_send.at[k], gm_recv.at[k], to_z(k)).wait_recv()
    for k in range(1, 8):
        remote(cd_s.at[0], cd_r.at[(pi - k + 8) % 8], c_send.at[k], c_recv.at[k], to_plane(k)).wait_recv()
    t0 = t1 = jnp.zeros((3, 128), F32)
    for b in range(8):
        zero_t[b, 0:3] = t0
        zero_t[b, 3:6] = t1
        n0, n1 = apply2(map_r[b], 0, t0, t1)
        t0, t1 = n0 + cd_r[b, 0:3, :], n1 + cd_r[b, 3:6, :]
    gcd_s[0:3] = t0
    gcd_s[3:6] = t1
    s0 = s1 = jnp.zeros((3, 128), F32)
    for b in range(7, -1, -1):
        zero_s[b, 0:3] = s0
        zero_s[b, 3:6] = s1
        w0, w1 = apply2(map_r[b], 4, zero_t[b, 0:3], zero_t[b, 3:6])
        u0, u1 = apply2(map_r[b], 8, s0, s1)
        s0, s1 = u0 + (w0 + cd_r[b, 6:9, :]), u1 + (w1 + cd_r[b, 9:12, :])
    gcd_s[6:9] = s0
    gcd_s[9:12] = s1

    for k in range(1, 8):
        copy = remote(gcd_s, gcd_r.at[zi], gc_send.at[k], gc_recv.at[k], to_z(k))
        copy.start()
        sends.append(copy)
    gcd_r[zi] = gcd_s[...]
    for k in range(1, 8):
        remote(gcd_s, gcd_r.at[(zi - k + 8) % 8], gc_send.at[k], gc_recv.at[k], to_z(k)).wait_recv()
    t0 = t1 = jnp.zeros((3, 128), F32)
    for g in range(8):
        t_in[g, 0:3] = t0
        t_in[g, 3:6] = t1
        n0, n1 = apply2(gmap_r[g], 0, t0, t1)
        t0, t1 = n0 + gcd_r[g, 0:3, :], n1 + gcd_r[g, 3:6, :]
    s0 = s1 = jnp.zeros((3, 128), F32)
    for g in range(7, -1, -1):
        s_in[g, 0:3] = s0
        s_in[g, 3:6] = s1
        w0, w1 = apply2(gmap_r[g], 4, t_in[g, 0:3], t_in[g, 3:6])
        u0, u1 = apply2(gmap_r[g], 8, s0, s1)
        s0, s1 = u0 + (w0 + gcd_r[g, 6:9, :]), u1 + (w1 + gcd_r[g, 9:12, :])

    t0, t1 = t_in[zi, 0:3], t_in[zi, 3:6]
    s0, s1 = s_in[zi, 0:3], s_in[zi, 3:6]

    def mapped(base, b, first, second):
        return (
            base[b, 0:1] * first + base[b, 1:2] * second,
            base[b, 2:3] * first + base[b, 3:4] * second,
        )

    for j in range(4):
        b = 2 * j + co
        a0, a1 = mapped(base_t, b, t0, t1)
        ts_s[j, 0:3] = zero_t[b, 0:3] + a0
        ts_s[j, 3:6] = zero_t[b, 3:6] + a1
        a0, a1 = mapped(base_s, b, t0, t1)
        b0, b1 = mapped(base_r, b, s0, s1)
        ts_s[j, 6:9] = zero_s[b, 0:3] + a0 + b0
        ts_s[j, 9:12] = zero_s[b, 3:6] + a1 + b1
    for k in range(1, 4):
        copy = remote(
            ts_s.at[(xj + k) % 4], ts_r.at[xj], ts_send.at[k], ts_recv.at[k], to_plane(2 * k)
        )
        copy.start()
        sends.append(copy)
    ts_r[xj] = ts_s[xj]
    for k in range(1, 4):
        remote(
            ts_s.at[0], ts_r.at[(xj - k + 4) % 4], ts_send.at[k], ts_recv.at[k], to_plane(2 * k)
        ).wait_recv()

    for lt in range(4):
        for f in range(3):
            value = local[lt, f]
            for k in range(2):
                value = value - spk_d[lt, k * 24 : k * 24 + 24, :] * ts_r[lt, 3 * k + f : 3 * k + f + 1, :]
            for k in range(2):
                value = value - spk_d[lt, 48 + k * 24 : 72 + k * 24, :] * ts_r[lt, 6 + 3 * k + f : 7 + 3 * k + f, :]
            out[f, :, lt * 128 : lt * 128 + 128] = value
    for copy in sends:
        copy.wait_send()


def per_device(velocity, explicit, bands, inverse, spikes):
    dma = pltpu.SemaphoreType.DMA
    vmem = lambda *shape: pltpu.VMEM(shape, F32)
    hbm = pl.BlockSpec(memory_space=pltpu.HBM)
    operands = [
        pltpu.with_memory_space_constraint(a, pltpu.HBM)
        for a in (velocity, explicit, bands.transpose(1, 0, 2), inverse.reshape(576, 256), spikes.reshape(96, 256))
    ]
    return pl.pallas_call(
        kernel,
        out_shape=jax.ShapeDtypeStruct((3, 24, 512), F32),
        in_specs=[hbm] * 5,
        out_specs=pl.BlockSpec(memory_space=pltpu.VMEM),
        scratch_shapes=[
            vmem(5, 2, 24),
            vmem(8, 3, 3, 512), vmem(8, 3, 3, 512), vmem(2, 3, 3, 512), vmem(2, 3, 3, 512),
            vmem(2, 576, 128), vmem(4, 24, 24, 128), vmem(2, 96, 128), vmem(4, 96, 128),
            vmem(10, 24, 128), vmem(4, 3, 32, 128), vmem(4, 3, 32, 128),
            vmem(4, 3, 24, 128), vmem(4, 3, 24, 128),
            vmem(4, 12, 128), vmem(8, 12, 128), vmem(12, 128), vmem(8, 12, 128),
            vmem(4, 12, 128), vmem(8, 12, 128), vmem(12, 128), vmem(8, 12, 128),
            vmem(8, 12, 128), vmem(4, 12, 128),
            vmem(8, 4, 128), vmem(8, 4, 128), vmem(8, 4, 128),
            vmem(8, 6, 128), vmem(8, 6, 128), vmem(8, 6, 128), vmem(8, 6, 128),
            dma((5,)), dma((2,)), dma((8,)), dma((8,)), dma((8,)), dma((8,)), dma((4,)), dma((4,)),
            dma((8,)), dma((8,)), dma((8,)), dma((8,)), dma((8,)), dma((8,)), dma((8,)), dma((8,)),
            dma((4,)), dma((4,)),
        ],
        compiler_params=pltpu.CompilerParams(collective_id=0, has_side_effects=True, vmem_limit_bytes=16 * 1024 * 1024),
    )(*operands)


def solution(mesh):
    placed = (
        P(None, ("gy", "gz"), None),
        P(None, ("gy", "gz"), None),
        P(None, None, "gy"),
        P("gy", None, "gz"),
        P(None, None, "gy", "gz"),
    )
    return jax.shard_map(
        per_device, mesh=mesh, in_specs=placed, out_specs=P(None, "gy", "gz"), check_vma=False
    )
```

```python
import functools

import jax
import jax.numpy as jnp
from jax import lax
from jax.experimental import pallas as pl
from jax.experimental.pallas import tpu as pltpu
from jax.sharding import PartitionSpec as P

MESH = pl.DeviceIdType.MESH
F32 = jnp.float32


def kernel(
    vel, exp, bands_in, inv, spk, out,
    bands, vs, es, rv, re, hv, he, inv_h, inv_t, spk_h, spk_d, coef, vx, ex, rhs, local,
    map_s, map_r, gmap_s, gmap_r, cd_s, cd_r, gcd_s, gcd_r, ts_s, ts_r,
    base_t, base_s, base_r, zero_t, zero_s, wp, wv, wq, zp, zv, zq,
    ld_sem, own_sem, rv_send, rv_recv, re_send, re_recv, h_send, h_recv,
    m_send, m_recv, gm_send, gm_recv, c_send, c_recv, gc_send, gc_recv, ts_send, ts_recv,
):
    gy = lax.axis_index("gy")
    gz = lax.axis_index("gz")
    zi = gy // 8
    pi = gy % 8
    half = pi // 4
    tile = pi % 4

    def to_y(k):
        return {"gz": (gz + k) % 8}

    def to_plane(k):
        return {"gy": zi * 8 + (pi + k) % 8}

    def to_half(k):
        return {"gy": zi * 8 + half * 4 + (tile + k) % 4}

    def to_z(k):
        return {"gy": ((zi + k) % 8) * 8 + pi}

    def to_next(k):
        return {"gy": (gy + k + 64) % 64}

    def remote(src, dst, send, recv, where):
        return pltpu.make_async_remote_copy(
            src_ref=src, dst_ref=dst, send_sem=send, recv_sem=recv,
            device_id=where, device_id_type=MESH,
        )

    planes = [
        pltpu.make_async_copy(vel, vs, ld_sem.at[5]),
        pltpu.make_async_copy(exp, es, ld_sem.at[6]),
    ]
    for copy in planes:
        copy.start()
    loads = []
    for h in range(2):
        loads.append(pltpu.make_async_copy(spk.at[:, pl.ds(h * 128, 128)], spk_h.at[h], ld_sem.at[h]))
    for h in range(2):
        loads.append(pltpu.make_async_copy(inv.at[:, pl.ds(h * 128, 128)], inv_h.at[h], ld_sem.at[2 + h]))
    loads.append(pltpu.make_async_copy(bands_in, bands, ld_sem.at[4]))
    for copy in loads:
        copy.start()
    barrier = pltpu.get_barrier_semaphore()
    for k in range(1, 8):
        for where in (to_y(k), to_z(k), to_plane(k)):
            pl.semaphore_signal(barrier, inc=1, device_id=where, device_id_type=MESH)
    for k in (-1, 1):
        pl.semaphore_signal(barrier, inc=1, device_id=to_next(k), device_id_type=MESH)
    pl.semaphore_wait(barrier, 23)

    for copy in planes:
        copy.wait()
    sends = []
    for k in (1, 7, 2, 6, 3, 5, 4):
        cols = pl.ds(pl.multiple_of(((gz + k) % 8) * 512, 512), 512)
        for src, dst, send, recv in ((vs, rv, rv_send, rv_recv), (es, re, re_send, re_recv)):
            copy = remote(src.at[:, :, cols], dst.at[gz], send.at[k], recv.at[k], to_y(k))
            copy.start()
            sends.append(copy)

    mine = pl.ds(pl.multiple_of(gz * 512, 512), 512)
    pltpu.make_async_copy(vs.at[:, :, mine], rv.at[gz], rv_recv.at[0]).start()
    pltpu.make_async_copy(es.at[:, :, mine], re.at[gz], re_recv.at[0]).start()

    lane = lax.broadcasted_iota(jnp.int32, (24, 128), 1) // 2
    for h in range(2):
        loads[h].wait()

    def double_spikes(i, carry):
        row = pl.multiple_of(i * 24, 8)
        for h in range(2):
            part = spk_h[h, pl.ds(row, 24), :]
            for j in range(2):
                spk_d[2 * h + j, pl.ds(row, 24), :] = jnp.take_along_axis(part, lane + 64 * j, axis=1)
        return carry

    lax.fori_loop(0, 4, double_spikes, 0)
    for lt in range(4):
        for k in range(2):
            for q in range(2):
                i = 2 * k + q
                map_s[lt, i : i + 1, :] = -spk_d[lt, q * 24 + 22 + k : q * 24 + 23 + k, :]
                map_s[lt, 4 + i : 5 + i, :] = -spk_d[lt, q * 24 + k : q * 24 + k + 1, :]
                map_s[lt, 8 + i : 9 + i, :] = -spk_d[lt, 48 + q * 24 + k : 48 + q * 24 + k + 1, :]
    map_r[pi] = map_s[tile]
    for k in range(1, 8):
        copy = remote(
            map_s.at[(pi + k) % 4], map_r.at[pi], m_send.at[k], m_recv.at[k], to_plane(k)
        )
        copy.start()
        sends.append(copy)

    eye = lax.broadcasted_iota(jnp.int32, (24, 24), 0) == lax.broadcasted_iota(jnp.int32, (24, 24), 1)
    loads[4].wait()
    for d in range(5):
        first = bands[d, 0:1, :]
        second = bands[d, 1:2, :]
        for i, row in ((d, first + second), (5 + d, first)):
            column = jnp.sum(jnp.where(eye, row, 0.0), axis=1, keepdims=True)
            coef[i] = jnp.broadcast_to(column, (24, 128))

    for h in range(2):
        loads[2 + h].wait()

    def turn(c, carry):
        for h in range(2):
            part = inv_h[h, pl.ds(c, 24, stride=24), :]
            for j in range(2):
                inv_t[2 * h + j, c] = jnp.take_along_axis(part, lane + 64 * j, axis=1)
        return carry

    lax.fori_loop(0, 24, turn, 0)

    def apply2(maps, at, first, second):
        return (
            maps[at : at + 1, :] * first + maps[at + 1 : at + 2, :] * second,
            maps[at + 2 : at + 3, :] * first + maps[at + 3 : at + 4, :] * second,
        )

    for k in range(1, 8):
        remote(map_s.at[0], map_r.at[(pi - k + 8) % 8], m_send.at[k], m_recv.at[k], to_plane(k)).wait_recv()
    col = lax.broadcasted_iota(jnp.int32, (2, 128), 0)
    unit = (jnp.where(col == 0, 1.0, 0.0), jnp.where(col == 1, 1.0, 0.0))
    t0, t1 = unit
    for b in range(8):
        base_t[b, 0:2] = t0
        base_t[b, 2:4] = t1
        t0, t1 = apply2(map_r[b], 0, t0, t1)
    s0 = s1 = jnp.zeros((2, 128), F32)
    r0, r1 = unit
    gmap_s[0:2] = t0
    gmap_s[2:4] = t1
    for b in range(7, -1, -1):
        maps = map_r[b]
        base_s[b, 0:2] = s0
        base_s[b, 2:4] = s1
        base_r[b, 0:2] = r0
        base_r[b, 2:4] = r1
        w0, w1 = apply2(maps, 4, base_t[b, 0:2], base_t[b, 2:4])
        u0, u1 = apply2(maps, 8, s0, s1)
        s0, s1 = w0 + u0, w1 + u1
        r0, r1 = apply2(maps, 8, r0, r1)
    gmap_s[4:6] = s0
    gmap_s[6:8] = s1
    gmap_s[8:10] = r0
    gmap_s[10:12] = r1
    gmap_r[zi] = gmap_s[...]
    for k in range(1, 8):
        copy = remote(gmap_s, gmap_r.at[zi], gm_send.at[k], gm_recv.at[k], to_z(k))
        copy.start()
        sends.append(copy)

    def weights(maps, hi, lo, p, v, q):
        def times(x, m, at):
            top, low = m[at : at + 2, :], m[at + 2 : at + 4, :]
            return [row[0:1] * top + row[1:2] * low for row in x]

        def put(where, x):
            where[0:2] = x[0]
            where[2:4] = x[1]

        x = [jnp.zeros((2, 128), F32)] * 2
        for g in range(8):
            if g > 0:
                x = times(x, maps[g - 1], 8)
            x = [jnp.where(g == lo + 1, one, row) for one, row in zip(unit, x)]
            put(q.at[g], x)
        x = [jnp.zeros((2, 128), F32)] * 2
        y = x
        for g in range(7, -1, -1):
            if g < 7:
                m = maps[g + 1]
                x = times(x, m, 0)
                after = (q[g + 1, 0:2], q[g + 1, 2:4])
                y = [a + b for a, b in zip(times(y, m, 0), times(after, m, 4))]
            x = [jnp.where(g == hi - 1, one, row) for one, row in zip(unit, x)]
            put(p.at[g], x)
            put(v.at[g], y)

    def gathered(p, v, q, got):
        t = [jnp.zeros((3, 128), F32)] * 2
        s = [jnp.zeros((3, 128), F32)] * 2
        for g in range(8):
            t_zero, t_one = got[g, 0:3, :], got[g, 3:6, :]
            s_zero, s_one = got[g, 6:9, :], got[g, 9:12, :]
            for k in range(2):
                i = 2 * k
                t[k] = t[k] + (p[g, i : i + 1] * t_zero + p[g, i + 1 : i + 2] * t_one)
                s[k] = s[k] + (
                    (v[g, i : i + 1] * t_zero + v[g, i + 1 : i + 2] * t_one)
                    + (q[g, i : i + 1] * s_zero + q[g, i + 1 : i + 2] * s_one)
                )
        return t, s

    def wait_slot(slot):
        k = (gz - slot + 8) % 8
        pltpu.make_async_copy(rv.at[slot], rv.at[slot], rv_recv.at[k]).wait()
        pltpu.make_async_copy(re.at[slot], re.at[slot], re_recv.at[k]).wait()

    halos = []
    for side, slot, step in ((0, 7, 1), (1, 0, -1)):
        wait_slot(slot)
        for a, (src, dst) in enumerate(((rv, hv), (re, he))):
            i = 2 * side + a
            copy = remote(src.at[slot], dst.at[side], h_send.at[i], h_recv.at[i], to_next(step))
            copy.start()
            sends.append(copy)
            halos.append(copy)

    weights(map_r, 8, -1, wp, wv, wq)

    def gather_rows(g):
        def body(lt, carry):
            cols = pl.ds(pl.multiple_of(lt * 128, 128), 128)
            for got, rows in ((rv, vx), (re, ex)):
                for f in range(3):
                    rows[lt, f, 2 + 3 * g : 5 + 3 * g, :] = got[g, f, :, cols]
            return carry

        lax.fori_loop(0, 4, body, 0)

    gather_rows(7)
    gather_rows(0)
    for g in (3, 4, 2, 5, 1, 6):
        wait_slot(g)
        gather_rows(g)
    for copy in halos:
        copy.wait_recv()

    def gather_edges(lt, carry):
        cols = pl.ds(pl.multiple_of(lt * 128, 128), 128)
        for got, rows in ((hv, vx), (he, ex)):
            for f in range(3):
                rows[lt, f, 0:2, :] = jnp.where(gy > 0, got[0, f, 1:3, cols], 0.0)
                rows[lt, f, 26:28, :] = jnp.where(gy < 63, got[1, f, 0:2, cols], 0.0)
        return carry

    lax.fori_loop(0, 4, gather_edges, 0)

    def solve(lt, carry):
        for f in range(3):
            total = jnp.zeros((24, 128), F32)
            for d in range(5):
                total = total + coef[d] * vx[lt, f, d : d + 24, :]
                total = total + coef[5 + d] * ex[lt, f, d : d + 24, :]
            rhs[lt, f] = total
        sums = [jnp.zeros((24, 128), F32) for _ in range(3)]
        for c in range(24):
            weight = inv_t[lt, c]
            for f in range(3):
                sums[f] = sums[f] + weight * rhs[lt, f, c : c + 1, :]
        for f in range(3):
            local[lt, f] = sums[f]
            for k in range(2):
                cd_s[lt, 3 * k + f : 3 * k + f + 1, :] = sums[f][22 + k : 23 + k, :]
                cd_s[lt, 6 + 3 * k + f : 7 + 3 * k + f, :] = sums[f][k : k + 1, :]
        return carry

    lax.fori_loop(0, 4, solve, 0)

    for k in range(1, 8):
        copy = remote(
            cd_s.at[(pi + k) % 4], cd_r.at[pi], c_send.at[k], c_recv.at[k], to_plane(k)
        )
        copy.start()
        sends.append(copy)
    cd_r[pi] = cd_s[tile]
    for k in range(1, 8):
        remote(gmap_s, gmap_r.at[(zi - k + 8) % 8], gm_send.at[k], gm_recv.at[k], to_z(k)).wait_recv()
    weights(gmap_r, zi, zi, zp, zv, zq)
    for k in range(1, 8):
        remote(cd_s.at[0], cd_r.at[(pi - k + 8) % 8], c_send.at[k], c_recv.at[k], to_plane(k)).wait_recv()
    t, s = gathered(wp, wv, wq, cd_r)
    for k in range(2):
        gcd_s[3 * k : 3 * k + 3] = t[k]
        gcd_s[6 + 3 * k : 9 + 3 * k] = s[k]

    for k in range(1, 8):
        copy = remote(gcd_s, gcd_r.at[zi], gc_send.at[k], gc_recv.at[k], to_z(k))
        copy.start()
        sends.append(copy)
    gcd_r[zi] = gcd_s[...]
    t0 = t1 = jnp.zeros((3, 128), F32)
    for b in range(8):
        zero_t[b, 0:3] = t0
        zero_t[b, 3:6] = t1
        n0, n1 = apply2(map_r[b], 0, t0, t1)
        t0, t1 = n0 + cd_r[b, 0:3, :], n1 + cd_r[b, 3:6, :]
    s0 = s1 = jnp.zeros((3, 128), F32)
    for b in range(7, -1, -1):
        zero_s[b, 0:3] = s0
        zero_s[b, 3:6] = s1
        w0, w1 = apply2(map_r[b], 4, zero_t[b, 0:3], zero_t[b, 3:6])
        u0, u1 = apply2(map_r[b], 8, s0, s1)
        s0, s1 = u0 + (w0 + cd_r[b, 6:9, :]), u1 + (w1 + cd_r[b, 9:12, :])
    for k in range(1, 8):
        remote(gcd_s, gcd_r.at[(zi - k + 8) % 8], gc_send.at[k], gc_recv.at[k], to_z(k)).wait_recv()
    (t0, t1), (s0, s1) = gathered(zp, zv, zq, gcd_r)


    def mapped(base, b, first, second):
        return (
            base[b, 0:1] * first + base[b, 1:2] * second,
            base[b, 2:3] * first + base[b, 3:4] * second,
        )

    for j in range(4):
        b = 4 * half + j
        a0, a1 = mapped(base_t, b, t0, t1)
        ts_s[j, 0:3] = zero_t[b, 0:3] + a0
        ts_s[j, 3:6] = zero_t[b, 3:6] + a1
        a0, a1 = mapped(base_s, b, t0, t1)
        b0, b1 = mapped(base_r, b, s0, s1)
        ts_s[j, 6:9] = zero_s[b, 0:3] + a0 + b0
        ts_s[j, 9:12] = zero_s[b, 3:6] + a1 + b1
    for k in range(1, 4):
        copy = remote(
            ts_s.at[(tile + k) % 4], ts_r.at[tile], ts_send.at[k], ts_recv.at[k], to_half(k)
        )
        copy.start()
        sends.append(copy)
    ts_r[tile] = ts_s[tile]
    for k in range(1, 4):
        remote(
            ts_s.at[0], ts_r.at[(tile - k + 4) % 4], ts_send.at[k], ts_recv.at[k], to_half(k)
        ).wait_recv()

    for lt in range(4):
        for f in range(3):
            value = local[lt, f]
            for k in range(2):
                value = value - spk_d[lt, k * 24 : k * 24 + 24, :] * ts_r[lt, 3 * k + f : 3 * k + f + 1, :]
            for k in range(2):
                value = value - spk_d[lt, 48 + k * 24 : 72 + k * 24, :] * ts_r[lt, 6 + 3 * k + f : 7 + 3 * k + f, :]
            out[f, :, lt * 128 : lt * 128 + 128] = value
    for copy in sends:
        copy.wait_send()


def per_device(velocity, explicit, bands, inverse, spikes):
    dma = pltpu.SemaphoreType.DMA
    vmem = lambda *shape: pltpu.VMEM(shape, F32)
    hbm = pl.BlockSpec(memory_space=pltpu.HBM)
    operands = [
        pltpu.with_memory_space_constraint(a, pltpu.HBM)
        for a in (velocity, explicit, bands.transpose(1, 0, 2), inverse.reshape(576, 256), spikes.reshape(96, 256))
    ]
    return pl.pallas_call(
        kernel,
        out_shape=jax.ShapeDtypeStruct((3, 24, 512), F32),
        in_specs=[hbm] * 5,
        out_specs=pl.BlockSpec(memory_space=pltpu.VMEM),
        scratch_shapes=[
            vmem(5, 2, 24), vmem(3, 3, 4096), vmem(3, 3, 4096),
            vmem(8, 3, 3, 512), vmem(8, 3, 3, 512), vmem(2, 3, 3, 512), vmem(2, 3, 3, 512),
            vmem(2, 576, 128), vmem(4, 24, 24, 128), vmem(2, 96, 128), vmem(4, 96, 128),
            vmem(10, 24, 128), vmem(4, 3, 32, 128), vmem(4, 3, 32, 128),
            vmem(4, 3, 24, 128), vmem(4, 3, 24, 128),
            vmem(4, 12, 128), vmem(8, 12, 128), vmem(12, 128), vmem(8, 12, 128),
            vmem(4, 12, 128), vmem(8, 12, 128), vmem(12, 128), vmem(8, 12, 128),
            vmem(8, 12, 128), vmem(4, 12, 128),
            vmem(8, 4, 128), vmem(8, 4, 128), vmem(8, 4, 128),
            vmem(8, 6, 128), vmem(8, 6, 128), *[vmem(8, 4, 128) for _ in range(6)],
            dma((7,)), dma((2,)), dma((8,)), dma((8,)), dma((8,)), dma((8,)), dma((4,)), dma((4,)),
            dma((8,)), dma((8,)), dma((8,)), dma((8,)), dma((8,)), dma((8,)), dma((8,)), dma((8,)),
            dma((4,)), dma((4,)),
        ],
        compiler_params=pltpu.CompilerParams(collective_id=0, has_side_effects=True, vmem_limit_bytes=16 * 1024 * 1024),
    )(*operands)


def solution(mesh):
    placed = (
        P(None, ("gy", "gz"), None),
        P(None, ("gy", "gz"), None),
        P(None, None, "gy"),
        P("gy", None, "gz"),
        P(None, None, "gy", "gz"),
    )
    return jax.shard_map(
        per_device, mesh=mesh, in_specs=placed, out_specs=P(None, "gy", "gz"), check_vma=False
    )
```

```python
import functools

import jax
import jax.numpy as jnp
from jax import lax
from jax.experimental import pallas as pl
from jax.experimental.pallas import tpu as pltpu
from jax.sharding import PartitionSpec as P

MESH = pl.DeviceIdType.MESH
F32 = jnp.float32


def kernel(
    vel, exp, bands_in, inv, spk, out,
    bands, own, got, edge, inv_h, inv_t, spk_h, spk_d, coef, vx, ex, rhs, local,
    map_s, map_r, gmap_s, gmap_r, cd_s, cd_r, gcd_s, gcd_r, ts_s, ts_r,
    base_t, base_s, base_r, zero_t, zero_s, wp, wv, wq, zp, zv, zq,
    ld_sem, got_send, got_recv, h_send, h_recv,
    m_send, m_recv, gm_send, gm_recv, c_send, c_recv, gc_send, gc_recv, ts_send, ts_recv,
):
    gy = lax.axis_index("gy")
    gz = lax.axis_index("gz")
    zi = gy // 8
    pi = gy % 8
    half = pi // 4
    tile = pi % 4

    def to_y(k):
        return {"gz": (gz + k) % 8}

    def to_plane(k):
        return {"gy": zi * 8 + (pi + k) % 8}

    def to_half(k):
        return {"gy": zi * 8 + half * 4 + (tile + k) % 4}

    def to_z(k):
        return {"gy": ((zi + k) % 8) * 8 + pi}

    def to_next(k):
        return {"gy": (gy + k + 64) % 64}

    def remote(src, dst, send, recv, where):
        return pltpu.make_async_remote_copy(
            src_ref=src, dst_ref=dst, send_sem=send, recv_sem=recv,
            device_id=where, device_id_type=MESH,
        )

    barrier = pltpu.get_barrier_semaphore()
    for k in (4, 3, 5, 2, 6, 1, 7):
        for where in (to_y(k), to_z(k), to_plane(k)):
            pl.semaphore_signal(barrier, inc=1, device_id=where, device_id_type=MESH)
    for k in (-1, 1):
        pl.semaphore_signal(barrier, inc=1, device_id=to_next(k), device_id_type=MESH)
    planes = [
        pltpu.make_async_copy(vel, own.at[0], ld_sem.at[5]),
        pltpu.make_async_copy(exp, own.at[1], ld_sem.at[6]),
    ]
    for copy in planes:
        copy.start()
    loads = []
    for h in range(2):
        loads.append(pltpu.make_async_copy(spk.at[:, pl.ds(h * 128, 128)], spk_h.at[h], ld_sem.at[h]))
    for h in range(2):
        loads.append(pltpu.make_async_copy(inv.at[:, pl.ds(h * 128, 128)], inv_h.at[h], ld_sem.at[2 + h]))
    loads.append(pltpu.make_async_copy(bands_in, bands, ld_sem.at[4]))
    for copy in loads:
        copy.start()
    pl.semaphore_wait(barrier, 23)

    for copy in planes:
        copy.wait()
    sends = []
    for k in (1, 7, 2, 6, 3, 5, 4):
        cols = pl.ds(pl.multiple_of(((gz + k) % 8) * 512, 512), 512)
        copy = remote(own.at[:, :, :, cols], got.at[gz], got_send.at[k], got_recv.at[k], to_y(k))
        copy.start()
        sends.append(copy)
    mine = pl.ds(pl.multiple_of(gz * 512, 512), 512)
    pltpu.make_async_copy(own.at[:, :, :, mine], got.at[gz], got_recv.at[0]).start()

    lane = lax.broadcasted_iota(jnp.int32, (24, 128), 1) // 2
    for h in range(2):
        loads[h].wait()

    def double_spikes(i, carry):
        row = pl.multiple_of(i * 24, 8)
        for h in range(2):
            part = spk_h[h, pl.ds(row, 24), :]
            for j in range(2):
                spk_d[2 * h + j, pl.ds(row, 24), :] = jnp.take_along_axis(part, lane + 64 * j, axis=1)
        return carry

    lax.fori_loop(0, 4, double_spikes, 0)
    for lt in range(4):
        for k in range(2):
            for q in range(2):
                i = 2 * k + q
                map_s[lt, i : i + 1, :] = -spk_d[lt, q * 24 + 22 + k : q * 24 + 23 + k, :]
                map_s[lt, 4 + i : 5 + i, :] = -spk_d[lt, q * 24 + k : q * 24 + k + 1, :]
                map_s[lt, 8 + i : 9 + i, :] = -spk_d[lt, 48 + q * 24 + k : 48 + q * 24 + k + 1, :]
    map_r[pi] = map_s[tile]
    for k in range(1, 8):
        copy = remote(
            map_s.at[(pi + k) % 4], map_r.at[pi], m_send.at[k], m_recv.at[k], to_plane(k)
        )
        copy.start()
        sends.append(copy)

    eye = lax.broadcasted_iota(jnp.int32, (24, 24), 0) == lax.broadcasted_iota(jnp.int32, (24, 24), 1)
    loads[4].wait()
    for d in range(5):
        first = bands[d, 0:1, :]
        second = bands[d, 1:2, :]
        for i, row in ((d, first + second), (5 + d, first)):
            column = jnp.sum(jnp.where(eye, row, 0.0), axis=1, keepdims=True)
            coef[i] = jnp.broadcast_to(column, (24, 128))

    for h in range(2):
        loads[2 + h].wait()

    def turn(c, carry):
        for h in range(2):
            part = inv_h[h, pl.ds(c, 24, stride=24), :]
            for j in range(2):
                inv_t[2 * h + j, c] = jnp.take_along_axis(part, lane + 64 * j, axis=1)
        return carry

    lax.fori_loop(0, 24, turn, 0)

    def apply2(maps, at, first, second):
        return (
            maps[at : at + 1, :] * first + maps[at + 1 : at + 2, :] * second,
            maps[at + 2 : at + 3, :] * first + maps[at + 3 : at + 4, :] * second,
        )

    for k in range(1, 8):
        remote(map_s.at[0], map_r.at[(pi - k + 8) % 8], m_send.at[k], m_recv.at[k], to_plane(k)).wait_recv()
    col = lax.broadcasted_iota(jnp.int32, (2, 128), 0)
    unit = (jnp.where(col == 0, 1.0, 0.0), jnp.where(col == 1, 1.0, 0.0))
    t0, t1 = unit
    for b in range(8):
        base_t[b, 0:2] = t0
        base_t[b, 2:4] = t1
        t0, t1 = apply2(map_r[b], 0, t0, t1)
    s0 = s1 = jnp.zeros((2, 128), F32)
    r0, r1 = unit
    gmap_s[0:2] = t0
    gmap_s[2:4] = t1
    for b in range(7, -1, -1):
        maps = map_r[b]
        base_s[b, 0:2] = s0
        base_s[b, 2:4] = s1
        base_r[b, 0:2] = r0
        base_r[b, 2:4] = r1
        w0, w1 = apply2(maps, 4, base_t[b, 0:2], base_t[b, 2:4])
        u0, u1 = apply2(maps, 8, s0, s1)
        s0, s1 = w0 + u0, w1 + u1
        r0, r1 = apply2(maps, 8, r0, r1)
    gmap_s[4:6] = s0
    gmap_s[6:8] = s1
    gmap_s[8:10] = r0
    gmap_s[10:12] = r1
    gmap_r[zi] = gmap_s[...]
    for k in range(1, 8):
        copy = remote(gmap_s, gmap_r.at[zi], gm_send.at[k], gm_recv.at[k], to_z(k))
        copy.start()
        sends.append(copy)

    def weights(maps, hi, lo, p, v, q):
        def times(x, m, at):
            top, low = m[at : at + 2, :], m[at + 2 : at + 4, :]
            return [row[0:1] * top + row[1:2] * low for row in x]

        def put(where, x):
            where[0:2] = x[0]
            where[2:4] = x[1]

        x = [jnp.zeros((2, 128), F32)] * 2
        for g in range(8):
            if g > 0:
                x = times(x, maps[g - 1], 8)
            x = [jnp.where(g == lo + 1, one, row) for one, row in zip(unit, x)]
            put(q.at[g], x)
        x = [jnp.zeros((2, 128), F32)] * 2
        y = x
        for g in range(7, -1, -1):
            if g < 7:
                m = maps[g + 1]
                x = times(x, m, 0)
                after = (q[g + 1, 0:2], q[g + 1, 2:4])
                y = [a + b for a, b in zip(times(y, m, 0), times(after, m, 4))]
            x = [jnp.where(g == hi - 1, one, row) for one, row in zip(unit, x)]
            put(p.at[g], x)
            put(v.at[g], y)

    def gathered(p, v, q, got):
        t = [jnp.zeros((3, 128), F32)] * 2
        s = [jnp.zeros((3, 128), F32)] * 2
        for g in range(8):
            t_zero, t_one = got[g, 0:3, :], got[g, 3:6, :]
            s_zero, s_one = got[g, 6:9, :], got[g, 9:12, :]
            for k in range(2):
                i = 2 * k
                t[k] = t[k] + (p[g, i : i + 1] * t_zero + p[g, i + 1 : i + 2] * t_one)
                s[k] = s[k] + (
                    (v[g, i : i + 1] * t_zero + v[g, i + 1 : i + 2] * t_one)
                    + (q[g, i : i + 1] * s_zero + q[g, i + 1 : i + 2] * s_one)
                )
        return t, s

    def wait_slot(slot):
        k = (gz - slot + 8) % 8
        pltpu.make_async_copy(got.at[slot], got.at[slot], got_recv.at[k]).wait()

    halos = []
    for side, slot, step in ((0, 7, 1), (1, 0, -1)):
        wait_slot(slot)
        copy = remote(got.at[slot], edge.at[side], h_send.at[side], h_recv.at[side], to_next(step))
        copy.start()
        sends.append(copy)
        halos.append(copy)

    weights(map_r, 8, -1, wp, wv, wq)

    def gather_rows(g):
        def body(lt, carry):
            cols = pl.ds(pl.multiple_of(lt * 128, 128), 128)
            for a, rows in ((0, vx), (1, ex)):
                for f in range(3):
                    rows[lt, f, 2 + 3 * g : 5 + 3 * g, :] = got[g, a, f, :, cols]
            return carry

        lax.fori_loop(0, 4, body, 0)

    gather_rows(7)
    gather_rows(0)
    for g in (3, 4, 2, 5, 1, 6):
        wait_slot(g)
        gather_rows(g)
    for copy in halos:
        copy.wait_recv()

    def gather_edges(lt, carry):
        cols = pl.ds(pl.multiple_of(lt * 128, 128), 128)
        for a, rows in ((0, vx), (1, ex)):
            for f in range(3):
                rows[lt, f, 0:2, :] = jnp.where(gy > 0, edge[0, a, f, 1:3, cols], 0.0)
                rows[lt, f, 26:28, :] = jnp.where(gy < 63, edge[1, a, f, 0:2, cols], 0.0)
        return carry

    lax.fori_loop(0, 4, gather_edges, 0)

    def solve(lt, carry):
        for f in range(3):
            total = jnp.zeros((24, 128), F32)
            for d in range(5):
                total = total + coef[d] * vx[lt, f, d : d + 24, :]
                total = total + coef[5 + d] * ex[lt, f, d : d + 24, :]
            rhs[lt, f] = total
        sums = [jnp.zeros((24, 128), F32) for _ in range(3)]
        for c in range(24):
            weight = inv_t[lt, c]
            for f in range(3):
                sums[f] = sums[f] + weight * rhs[lt, f, c : c + 1, :]
        for f in range(3):
            local[lt, f] = sums[f]
            for k in range(2):
                cd_s[lt, 3 * k + f : 3 * k + f + 1, :] = sums[f][22 + k : 23 + k, :]
                cd_s[lt, 6 + 3 * k + f : 7 + 3 * k + f, :] = sums[f][k : k + 1, :]
        return carry

    lax.fori_loop(0, 4, solve, 0)

    for k in range(1, 8):
        copy = remote(
            cd_s.at[(pi + k) % 4], cd_r.at[pi], c_send.at[k], c_recv.at[k], to_plane(k)
        )
        copy.start()
        sends.append(copy)
    cd_r[pi] = cd_s[tile]
    for k in range(1, 8):
        remote(gmap_s, gmap_r.at[(zi - k + 8) % 8], gm_send.at[k], gm_recv.at[k], to_z(k)).wait_recv()
    weights(gmap_r, zi, zi, zp, zv, zq)
    for k in range(1, 8):
        remote(cd_s.at[0], cd_r.at[(pi - k + 8) % 8], c_send.at[k], c_recv.at[k], to_plane(k)).wait_recv()
    t, s = gathered(wp, wv, wq, cd_r)
    for k in range(2):
        gcd_s[3 * k : 3 * k + 3] = t[k]
        gcd_s[6 + 3 * k : 9 + 3 * k] = s[k]

    for k in range(1, 8):
        copy = remote(gcd_s, gcd_r.at[zi], gc_send.at[k], gc_recv.at[k], to_z(k))
        copy.start()
        sends.append(copy)
    gcd_r[zi] = gcd_s[...]
    t0 = t1 = jnp.zeros((3, 128), F32)
    for b in range(8):
        zero_t[b, 0:3] = t0
        zero_t[b, 3:6] = t1
        n0, n1 = apply2(map_r[b], 0, t0, t1)
        t0, t1 = n0 + cd_r[b, 0:3, :], n1 + cd_r[b, 3:6, :]
    s0 = s1 = jnp.zeros((3, 128), F32)
    for b in range(7, -1, -1):
        zero_s[b, 0:3] = s0
        zero_s[b, 3:6] = s1
        w0, w1 = apply2(map_r[b], 4, zero_t[b, 0:3], zero_t[b, 3:6])
        u0, u1 = apply2(map_r[b], 8, s0, s1)
        s0, s1 = u0 + (w0 + cd_r[b, 6:9, :]), u1 + (w1 + cd_r[b, 9:12, :])
    for k in range(1, 8):
        remote(gcd_s, gcd_r.at[(zi - k + 8) % 8], gc_send.at[k], gc_recv.at[k], to_z(k)).wait_recv()
    (t0, t1), (s0, s1) = gathered(zp, zv, zq, gcd_r)


    def mapped(base, b, first, second):
        return (
            base[b, 0:1] * first + base[b, 1:2] * second,
            base[b, 2:3] * first + base[b, 3:4] * second,
        )

    for j in range(4):
        b = 4 * half + j
        a0, a1 = mapped(base_t, b, t0, t1)
        ts_s[j, 0:3] = zero_t[b, 0:3] + a0
        ts_s[j, 3:6] = zero_t[b, 3:6] + a1
        a0, a1 = mapped(base_s, b, t0, t1)
        b0, b1 = mapped(base_r, b, s0, s1)
        ts_s[j, 6:9] = zero_s[b, 0:3] + a0 + b0
        ts_s[j, 9:12] = zero_s[b, 3:6] + a1 + b1
    for k in range(1, 4):
        copy = remote(
            ts_s.at[(tile + k) % 4], ts_r.at[tile], ts_send.at[k], ts_recv.at[k], to_half(k)
        )
        copy.start()
        sends.append(copy)
    ts_r[tile] = ts_s[tile]
    for k in range(1, 4):
        remote(
            ts_s.at[0], ts_r.at[(tile - k + 4) % 4], ts_send.at[k], ts_recv.at[k], to_half(k)
        ).wait_recv()

    for lt in range(4):
        for f in range(3):
            value = local[lt, f]
            for k in range(2):
                value = value - spk_d[lt, k * 24 : k * 24 + 24, :] * ts_r[lt, 3 * k + f : 3 * k + f + 1, :]
            for k in range(2):
                value = value - spk_d[lt, 48 + k * 24 : 72 + k * 24, :] * ts_r[lt, 6 + 3 * k + f : 7 + 3 * k + f, :]
            out[f, :, lt * 128 : lt * 128 + 128] = value
    for copy in sends:
        copy.wait_send()


def per_device(velocity, explicit, bands, inverse, spikes):
    dma = pltpu.SemaphoreType.DMA
    vmem = lambda *shape: pltpu.VMEM(shape, F32)
    hbm = pl.BlockSpec(memory_space=pltpu.HBM)
    operands = [
        pltpu.with_memory_space_constraint(a, pltpu.HBM)
        for a in (velocity, explicit, bands.transpose(1, 0, 2), inverse.reshape(576, 256), spikes.reshape(96, 256))
    ]
    return pl.pallas_call(
        kernel,
        out_shape=jax.ShapeDtypeStruct((3, 24, 512), F32),
        in_specs=[hbm] * 5,
        out_specs=pl.BlockSpec(memory_space=pltpu.VMEM),
        scratch_shapes=[
            vmem(5, 2, 24), vmem(2, 3, 3, 4096),
            vmem(8, 2, 3, 3, 512), vmem(2, 2, 3, 3, 512),
            vmem(2, 576, 128), vmem(4, 24, 24, 128), vmem(2, 96, 128), vmem(4, 96, 128),
            vmem(10, 24, 128), vmem(4, 3, 32, 128), vmem(4, 3, 32, 128),
            vmem(4, 3, 24, 128), vmem(4, 3, 24, 128),
            vmem(4, 12, 128), vmem(8, 12, 128), vmem(12, 128), vmem(8, 12, 128),
            vmem(4, 12, 128), vmem(8, 12, 128), vmem(12, 128), vmem(8, 12, 128),
            vmem(8, 12, 128), vmem(4, 12, 128),
            vmem(8, 4, 128), vmem(8, 4, 128), vmem(8, 4, 128),
            vmem(8, 6, 128), vmem(8, 6, 128), *[vmem(8, 4, 128) for _ in range(6)],
            dma((7,)), dma((8,)), dma((8,)), dma((2,)), dma((2,)),
            dma((8,)), dma((8,)), dma((8,)), dma((8,)), dma((8,)), dma((8,)), dma((8,)), dma((8,)),
            dma((4,)), dma((4,)),
        ],
        compiler_params=pltpu.CompilerParams(collective_id=0, has_side_effects=True, vmem_limit_bytes=16 * 1024 * 1024),
    )(*operands)


def solution(mesh):
    placed = (
        P(None, ("gy", "gz"), None),
        P(None, ("gy", "gz"), None),
        P(None, None, "gy"),
        P("gy", None, "gz"),
        P(None, None, "gy", "gz"),
    )
    return jax.shard_map(
        per_device, mesh=mesh, in_specs=placed, out_specs=P(None, "gy", "gz"), check_vma=False
    )
```
